256 devices in a mesh: rows: 16 (over x_lo, y, core), section: 16 (over z, x_hi).
Axes of the slice: x: 4 (x_hi: 2, x_lo: 2; x = x_hi * 2 + x_lo), y: 4, z: 8, core: 2. Of those that a mesh axis runs over, the one named last changes fastest.
Arguments:
- x_blocks: bfloat16 [192, 16, 2, 128, 128], P('rows', 'section'), may hold values from -2 to 2
- x_cols: int32 [192, 16], P('rows', 'section'), may hold values from -1 to 11, as said below
- c_cols: int32 [192, 48], P('rows', 'section'), may hold values from 0 to 11, as said below
- c_keep: int32 [192, 48], P('rows', 'section'), may hold values 0 or 1
Outputs:
- squared: bfloat16 [192, 48, 2, 128, 128], P('rows', 'section')
The draws below stay inside these ranges and needn't reach their ends.
Inputs may be any that keep to these rules, and one draw needn't show every extreme that they name: `x_cols`: for each block row and panel, the non-empty entries among its 1 slots name distinct columns of the panel; the share of empty slots differs from block row to block row. `c_cols`: for each block row and panel, its 3 entries name distinct columns of the panel.
All inputs are finite; a program needn't handle non-finite values. No bound on the sum of `c_keep` on one device may be relied on, other than what follows from the above.
Results may differ from the reference program's by a relative error of at most 0.001.
Values may be sent and summed in bfloat16 or wider, within the bound.
A program may use at most 128 MiB of HBM per device.

```python
import jax
import jax.numpy as jnp
from jax import lax

BS = 128
L = 1
LC = 3
NB = 192
PB = 12
NSL = 16
NSC = 48
N_SECTION = 16


def distinct_columns(key, per_panel):
    scores = jax.random.randint(key, (NB, NSL // L, PB), 0, 1 << 16, dtype=jnp.int32) * PB + jnp.arange(PB, dtype=jnp.int32)
    values_unused, picked = lax.top_k(scores, per_panel)
    return picked.reshape(NB, NSL // L * per_panel).astype(jnp.int32)


def stored_columns(key):
    column = distinct_columns(jax.random.fold_in(key, 11), L)
    level = jax.random.randint(jax.random.fold_in(key, 12), (NB, 1), 0, 3, dtype=jnp.int32)
    chance = jax.random.randint(jax.random.fold_in(key, 13), (NB, NSL), 0, 8, dtype=jnp.int32)
    return jnp.where(chance < 2 * level, -1, column).astype(jnp.int32)


def draw_x_cols(key, part):
    return stored_columns(key)


def draw_c_cols(key, part):
    stored = stored_columns(key)
    panels = NSL // L
    slot_ids = jnp.arange(NSL, dtype=jnp.int32)
    present = stored >= 0
    reach_rows = jnp.where(present, (slot_ids // L)[None, :] * PB + stored, 0).astype(jnp.int32)
    far_cols = stored[reach_rows].reshape(NB, NSL, panels, L)
    column_ids = jnp.arange(PB, dtype=jnp.int32)
    reached = (far_cols[:, :, :, :, None] == column_ids) & present[:, :, None, None, None]
    counts = jnp.sum(reached.astype(jnp.int32), axis=(1, 3))
    noise = jax.random.randint(jax.random.fold_in(key, 21), (NB, panels, PB), 0, 4096, dtype=jnp.int32)
    scores = (counts * 4096 + noise) * PB + column_ids
    values_unused, picked = lax.top_k(scores, LC)
    return picked.reshape(NB, panels * LC).astype(jnp.int32)


def set_ends(array, key, low, largest):
    longest = array.shape.index(max(array.shape))
    spots = []
    for shift in (0, 1):
        where = [jax.random.randint(jax.random.fold_in(key, axis), (), 0, length) for axis, length in enumerate(array.shape)]
        where[longest] = (where[longest] + shift) % array.shape[longest]
        spots.append(tuple(where))
    return array.at[spots[0]].set(low).at[spots[1]].set(largest)


def shard_levels(stream_key, extent, cuts, low, largest):
    level = 1.0
    for dim, shards_of in cuts:
        steps = jax.random.uniform(jax.random.fold_in(jax.random.fold_in(stream_key, 6), dim), (shards_of,), jnp.float32, low / len(cuts), largest / len(cuts))
        level = level * jnp.repeat(jnp.exp(steps), extent[dim] // shards_of).reshape((-1,) + (1,) * (len(extent) - 1 - dim))
    return level


def normal_values(own_key, dims, scale, most, shards=(), held_as=jnp.bfloat16):
    loudness = shard_levels(own_key, dims, shards, -0.22, 0.18) if shards else 1.0
    result = jax.random.normal(own_key, dims, jnp.float32) * scale * loudness
    return jnp.minimum(jnp.maximum(result, -most), most).astype(held_as)


def setup_inputs(seed: int = 0) -> dict:
    streams_of = jax.random.split(jax.random.key(seed), 5)
    x_blocks = normal_values(streams_of[0], (NB, NSL, 2, BS, BS), 0.155, 2.0, ((0, 16), (1, 16)))
    x_cols = draw_x_cols(jax.random.fold_in(streams_of[4], 71), 0)
    c_cols = draw_c_cols(jax.random.fold_in(streams_of[4], 71), 0)
    c_keep = set_ends((jax.random.randint(streams_of[3], (NB, NSC), 0, 4) < 3).astype(jnp.int32), jax.random.fold_in(streams_of[3], 1), 0, 1)
    return dict(x_blocks=x_blocks, x_cols=x_cols, c_cols=c_cols, c_keep=c_keep)


def reference(x_blocks, x_cols, c_cols, c_keep):
    slots = jnp.arange(NSL, dtype=jnp.int32)
    panel_of = slots // L

    def one_row(index):
        blocks = x_blocks[index].astype(jnp.float32)
        cols = x_cols[index]
        present = cols >= 0
        rows_needed = jnp.where(present, panel_of * PB + cols, 0).astype(jnp.int32)
        far_blocks = x_blocks[rows_needed].astype(jnp.float32).reshape(NSL, N_SECTION, L, 2, BS, BS)
        far_cols = x_cols[rows_needed].reshape(NSL, N_SECTION, L)
        wanted = c_cols[index].reshape(N_SECTION, LC)
        hits = (far_cols[:, :, None, :] == wanted[None, :, :, None]) & present[:, None, None, None]
        products = jnp.einsum("apxy,aslqyz->aslpqxz", blocks, far_blocks)
        real_part = products[:, :, :, 0, 0] - products[:, :, :, 1, 1]
        imag_part = products[:, :, :, 0, 1] + products[:, :, :, 1, 0]
        complex_terms = jnp.stack([real_part, imag_part], axis=3)
        routed = jnp.einsum("ascl,aslrxz->scrxz", hits.astype(jnp.float32), complex_terms, precision=lax.Precision.HIGHEST)
        return routed.reshape(NSC, 2, BS, BS)

    product = lax.map(one_row, jnp.arange(NB, dtype=jnp.int32))
    kept = c_keep.astype(jnp.float32)[:, :, None, None, None]
    return (product * kept).astype(jnp.bfloat16)
```

```python
import functools

import jax
import jax.numpy as jnp
from jax import lax
from jax.experimental import pallas as pl
from jax.experimental.pallas import tpu as pltpu
from jax.sharding import PartitionSpec as P

MESH = pl.DeviceIdType.MESH
NX, NY, NZ, NC = 4, 4, 8, 2
RB = 12
GROUPS = 16
BLK = 256
HALF = RB * BLK // 2
META = 16
ROWS = RB * BLK + META
LC = 3


def where_am_i():
    r, s = lax.axis_index("rows"), lax.axis_index("section")
    c = lax.rem(r, 2)
    y = lax.rem(r // 2, NY)
    x = lax.rem(s, 2) * 2 + r // 8
    return x, y, s // 2, c


def device(x, y, z, c):
    return ((lax.rem(x, 2) * NY + y) * 2 + c, z * 2 + x // 2)


def wrap(v, n):
    return lax.rem(v + n, n)


class Copies:
    def __init__(self, send):
        self.send, self.used, self.pending = send, 0, []

    def start(self, cond, src, dst, recv, to):
        copy = pltpu.make_async_remote_copy(
            src_ref=src, dst_ref=dst, send_sem=self.send.at[self.used], recv_sem=recv,
            device_id=to, device_id_type=MESH,
        )
        self.used += 1
        if cond is None:
            copy.start()
        else:
            pl.when(cond)(copy.start)
        self.pending.append((cond, copy))

    def finish(self):
        for cond, copy in self.pending:
            if cond is None:
                copy.wait_send()
            else:
                pl.when(cond)(copy.wait_send)


def enter(partners):
    barrier = pltpu.get_barrier_semaphore()
    for to in partners:
        pl.semaphore_signal(barrier, inc=1, device_id=to, device_id_type=MESH)
    pl.semaphore_wait(barrier, len(partners))


def gather_kernel(x_ref, m_ref, a_ref, b_ref, am_ref, bm_ref, send, recv_a, recv_b, local):
    x, y, z, c = where_am_i()
    h = x // 2
    home = c == h
    away = c != h
    xp, xm = wrap(x + 1, NX), wrap(x - 1, NX)
    yp, ym = wrap(y + 1, NY), wrap(y - 1, NY)
    zp, zm = wrap(z + 1, NZ), wrap(z - 1, NZ)
    sib = device(x, y, z, 1 - c)
    swap = device(wrap(x + 2, NX), y, z, 1 - c)
    to_xp, to_xm = device(xp, y, z, c), device(xm, y, z, c)
    to_yp, to_ym = device(x, yp, z, c), device(x, ym, z, c)
    to_zp, to_zm = device(x, y, zp, c), device(x, y, zm, c)
    enter([sib, swap, to_xp, to_xm, to_yp, to_ym, to_zp, to_zm])
    cp = Copies(send)

    def half(ref, slot, k):
        return ref.at[slot, pl.ds(0, HALF)] if k == 0 else ref.at[slot, pl.ds(HALF, ROWS - HALF)]

    def arrived(cond, ref, recv, slot, part=None):
        view = ref.at[slot] if part is None else half(ref, slot, part)
        sem = recv.at[slot, 0 if part is None else part]
        wait = pltpu.make_async_remote_copy(
            src_ref=view, dst_ref=view, send_sem=send.at[0], recv_sem=sem, device_id=sib, device_id_type=MESH
        ).wait_recv
        if cond is None:
            wait()
        else:
            pl.when(cond)(wait)

    def full(cond, ref, recv, slot, to):
        cp.start(cond, ref.at[slot], ref.at[slot], recv.at[slot, 0], to)

    def part(cond, ref, recv, slot, k, to):
        cp.start(cond, half(ref, slot, k), half(ref, slot, k), recv.at[slot, k], to)

    def group(lo, ys, core):
        return (lo * NY + ys) * 2 + core

    own = group(lax.rem(x, 2), y, c)
    own_sib = group(lax.rem(x, 2), y, 1 - c)
    a_own = 2 * z + c
    body = pl.ds(0, RB * BLK)
    tail = pl.ds(RB * BLK, META)

    mine = [
        pltpu.make_async_copy(x_ref, a_ref.at[a_own, body], local.at[0]),
        pltpu.make_async_copy(m_ref, a_ref.at[a_own, tail], local.at[1]),
        pltpu.make_async_copy(x_ref, b_ref.at[own, body], local.at[2]),
        pltpu.make_async_copy(m_ref, b_ref.at[own, tail], local.at[3]),
    ]

    @pl.when(home)
    def _():
        for m in mine:
            m.start()

    a_partner = 2 * z + (1 - c)
    cp.start(away, x_ref, a_ref.at[a_partner, body], recv_a.at[a_partner, 0], swap)
    cp.start(away, m_ref, a_ref.at[a_partner, tail], recv_a.at[a_partner, 1], swap)
    cp.start(away, x_ref, b_ref.at[own, body], recv_b.at[own, 0], sib)
    cp.start(away, m_ref, b_ref.at[own, tail], recv_b.at[own, 1], sib)

    def z_own(cond):
        full(cond, a_ref, recv_a, a_own, to_zp)
        full(cond, a_ref, recv_a, a_own, to_zm)
        full(cond, a_ref, recv_a, a_own, sib)

    def arrived_in_two(cond, ref, recv, slot):
        for view, k in ((body, 0), (tail, 1)):
            v = ref.at[slot, view]
            wait = pltpu.make_async_remote_copy(
                src_ref=v, dst_ref=v, send_sem=send.at[0], recv_sem=recv.at[slot, k],
                device_id=sib, device_id_type=MESH,
            ).wait_recv
            pl.when(cond)(wait)

    @pl.when(home)
    def _():
        for m in mine:
            m.wait()

    z_own(home)
    arrived_in_two(home, b_ref, recv_b, own_sib)
    here = lax.rem(x, 2)
    mine_x, mine_y = group(here, y, 0), group(here, y, 1)
    for slot, first, second in ((mine_x, (to_xp, to_xm), None), (mine_y, (to_yp, to_ym), None)):
        for to in first:
            full(home, b_ref, recv_b, slot, to)
    for to in (to_yp, to_ym):
        full(home, b_ref, recv_b, mine_x, to)
    for to in (to_xp, to_xm):
        full(home, b_ref, recv_b, mine_y, to)

    arrived_in_two(away, a_ref, recv_a, a_own)
    z_own(away)

    js = [wrap(x - 2 * c - lo, NX) for lo in (0, 1)]

    def y_sends(cond, slot):
        full(cond, b_ref, recv_b, slot, to_yp)
        full(cond, b_ref, recv_b, slot, to_ym)

    def x_sends(cond, slot):
        full(cond, b_ref, recv_b, slot, to_xp)
        full(cond, b_ref, recv_b, slot, to_xm)

    def ring(d):
        for zs, k, to in ((wrap(z - d, NZ), 0, to_zp), (wrap(z + d, NZ), 1, to_zm)):
            slot = 2 * zs + c
            arrived(None, a_ref, recv_a, slot)
            if d < 3:
                full(None, a_ref, recv_a, slot, to)
            else:
                part(None, a_ref, recv_a, slot, k, to)
            full(None, a_ref, recv_a, slot, sib)

    def x_pass(lo, slot):
        j = js[lo]
        for jj, k, to in ((1, 0, to_xp), (3, 1, to_xm)):
            arrived(j == jj, b_ref, recv_b, slot)
            part(j == jj, b_ref, recv_b, slot, k, to)

    for lo in (0, 1):
        slot = group(lo, y, 0)
        x_pass(lo, slot)
        y_sends((js[lo] == 1) | (js[lo] == 3), slot)
    for ys, k, to in ((ym, 0, to_yp), (yp, 1, to_ym)):
        slot = group(here, ys, 1)
        arrived(home, b_ref, recv_b, slot)
        part(home, b_ref, recv_b, slot, k, to)
        x_sends(home, slot)
    ring(1)
    for lo in (0, 1):
        slot = group(lo, y, 0)
        for k in (0, 1):
            arrived(js[lo] == 2, b_ref, recv_b, slot, k)
        y_sends(js[lo] == 2, slot)
    y2 = wrap(y + 2, NY)
    slot = group(here, y2, 1)
    for k in (0, 1):
        arrived(home, b_ref, recv_b, slot, k)
    x_sends(home, slot)
    ring(2)
    for lo in (0, 1):
        for ys, k, to in ((ym, 0, to_yp), (yp, 1, to_ym)):
            slot = group(lo, ys, 0)
            arrived(None, b_ref, recv_b, slot)
            part(None, b_ref, recv_b, slot, k, to)
        x_pass(lo, group(lo, y, 1))
        for ys in (ym, yp):
            x_pass(lo, group(lo, ys, 1))
    ring(3)
    for lo in (0, 1):
        x_pass(lo, group(lo, y2, 1))
    for lo in (0, 1):
        for k in (0, 1):
            arrived(None, b_ref, recv_b, group(lo, y2, 0), k)
            for ys in (y, ym, yp, y2):
                arrived(js[lo] == 2, b_ref, recv_b, group(lo, ys, 1), k)
    slot = 2 * wrap(z + 4, NZ) + c
    for k in (0, 1):
        arrived(None, a_ref, recv_a, slot, k)
        part(None, a_ref, recv_a, slot, k, sib)
    for d in range(NZ):
        slot = 2 * wrap(z + d, NZ) + 1 - c
        if d == 4:
            for k in (0, 1):
                arrived(None, a_ref, recv_a, slot, k)
        else:
            arrived(None, a_ref, recv_a, slot)
    tails = [
        pltpu.make_async_copy(a_ref.at[:, tail], am_ref, local.at[0]),
        pltpu.make_async_copy(b_ref.at[:, tail], bm_ref, local.at[1]),
    ]
    for t in tails:
        t.start()
    for t in tails:
        t.wait()
    cp.finish()


def gather(x, meta):
    shape = jax.ShapeDtypeStruct((GROUPS, ROWS, 128), jnp.bfloat16)
    tails = jax.ShapeDtypeStruct((GROUPS, META, 128), jnp.bfloat16)
    return pl.pallas_call(
        gather_kernel,
        out_shape=(shape, shape, tails, tails),
        in_specs=[pl.BlockSpec(memory_space=pl.ANY)] * 2,
        out_specs=(pl.BlockSpec(memory_space=pl.ANY),) * 4,
        scratch_shapes=[
            pltpu.SemaphoreType.DMA((96,)),
            pltpu.SemaphoreType.DMA((GROUPS, 2)),
            pltpu.SemaphoreType.DMA((GROUPS, 2)),
            pltpu.SemaphoreType.DMA((4,)),
        ],
        compiler_params=pltpu.CompilerParams(collective_id=0, has_side_effects=True),
        name="gather_strip_and_panel",
    )(x, meta)


def product_kernel(slot_ref, a_ref, b_ref, o_ref, acc):
    i = pl.program_id(0)
    for q in range(LC):
        acc[q] = jnp.zeros_like(acc[q])

    @pl.loop(0, GROUPS)
    def _(t):
        code = slot_ref[i, t]

        @pl.when(code >= 0)
        def _():
            m = code // LC
            q = code - m * LC
            a_re, a_im = a_ref[t, :128, :], a_ref[t, 128:, :]
            row = pl.multiple_of(m * BLK, BLK)
            b = b_ref[t, pl.ds(row, BLK), :]
            b_re, b_im = b[:128], b[128:]
            lhs = jnp.concatenate([a_re, a_im], axis=1)
            rhs = jnp.concatenate(
                [jnp.concatenate([b_re, b_im], axis=1), jnp.concatenate([-b_im, b_re], axis=1)], axis=0
            )
            acc[q] += jnp.dot(lhs, rhs, preferred_element_type=jnp.float32)

    for q in range(LC):
        o_ref[0, q, 0] = acc[q][:, :128].astype(jnp.bfloat16)
        o_ref[0, q, 1] = acc[q][:, 128:].astype(jnp.bfloat16)


def product(code, a, b):
    return pl.pallas_call(
        product_kernel,
        out_shape=jax.ShapeDtypeStruct((RB, LC, 2, 128, 128), jnp.bfloat16),
        grid_spec=pltpu.PrefetchScalarGridSpec(
            num_scalar_prefetch=1,
            grid=(RB,),
            in_specs=[
                pl.BlockSpec((GROUPS, BLK, 128), lambda i, code: (0, i, 0)),
                pl.BlockSpec((GROUPS, ROWS, 128), lambda i, code: (0, 0, 0), pipeline_mode=pl.Buffered(1)),
            ],
            out_specs=pl.BlockSpec((1, LC, 2, 128, 128), lambda i, code: (i, 0, 0, 0, 0)),
            scratch_shapes=[pltpu.VMEM((LC, 128, 256), jnp.float32)],
        ),
        compiler_params=pltpu.CompilerParams(
            dimension_semantics=("arbitrary",), vmem_limit_bytes=32 << 20
        ),
        name="matched_block_products",
    )(code, a, b)


def swap_kernel(n, p_ref, o_ref, mid, send, recv_mid, recv, local):
    x, y, z, c = where_am_i()
    h = x // 2
    home = c == h
    away = c != h
    xp, xm = wrap(x + 1, NX), wrap(x - 1, NX)
    to = [device(xp, y, z, c), device(xm, y, z, c)]
    on = [device(xp, y, z, 1 - c), device(xm, y, z, 1 - c)]
    enter(to + on)
    cp = Copies(send)
    step = RB // (2 * n)
    keep = pltpu.make_async_copy(p_ref, o_ref, local.at[0])
    pl.when(home)(keep.start)

    def wait(cond, view, sem):
        pl.when(cond)(
            pltpu.make_async_remote_copy(
                src_ref=view, dst_ref=view, send_sem=send.at[0], recv_sem=sem, device_id=to[0], device_id_type=MESH
            ).wait_recv
        )

    def rows(ref, d, k):
        return ref.at[pl.ds((d * n + k) * step, step)]

    for k in range(n):
        for d in (0, 1):
            cp.start(away, rows(p_ref, d, k), rows(mid, d, k), recv_mid.at[d, k], to[d])
    from_away = [c != xm // 2, c != xp // 2]
    for k in range(n):
        for d in (0, 1):
            wait(from_away[d], rows(mid, d, k), recv_mid.at[d, k])
            cp.start(from_away[d], rows(mid, d, k), rows(o_ref, d, k), recv.at[d, k], on[d])
    for k in range(n):
        for d in (0, 1):
            wait(away, rows(o_ref, d, k), recv.at[d, k])
    pl.when(home)(keep.wait)
    cp.finish()


def swap_back(p):
    n = 3
    out, unused = pl.pallas_call(
        functools.partial(swap_kernel, n),
        out_shape=(jax.ShapeDtypeStruct(p.shape, p.dtype),) * 2,
        in_specs=[pl.BlockSpec(memory_space=pl.ANY)],
        out_specs=(pl.BlockSpec(memory_space=pl.ANY),) * 2,
        scratch_shapes=[
            pltpu.SemaphoreType.DMA((4 * n,)),
            pltpu.SemaphoreType.DMA((2, n)),
            pltpu.SemaphoreType.DMA((2, n)),
            pltpu.SemaphoreType.DMA((1,)),
        ],
        compiler_params=pltpu.CompilerParams(collective_id=1, has_side_effects=True),
        name="swap_results",
    )(p)
    return out


def on_device(x_blocks, x_cols, c_cols, c_keep):
    x = x_blocks.reshape(RB * BLK, 128)
    wanted = jnp.where(c_keep != 0, c_cols, -2)
    meta = jnp.concatenate([x_cols.T, wanted.T], axis=0)
    meta = jnp.pad(meta, ((0, META - 1 - LC), (0, 128 - RB))).astype(jnp.bfloat16)
    a, b, a_meta, b_meta = gather(x, meta)
    a_meta = a_meta[:, :, :RB].astype(jnp.int32)
    b_meta = b_meta[:, :, :RB].astype(jnp.int32)
    a_cols = a_meta[:, 0]
    pick = a_cols[:, :, None] == jnp.arange(RB)[None, None, :]
    column = jnp.sum(jnp.where(pick, b_meta[:, 0][:, None, :] + 1, 0), axis=2) - 1
    mine = lax.dynamic_index_in_dim(a_meta, lax.axis_index("section") // 2 * 2 + lax.rem(lax.axis_index("rows"), 2), 0, False)
    hit = (column[None] == mine[1 : 1 + LC][:, None, :]) & (column >= 0)[None]
    q = jnp.sum(jnp.where(hit, jnp.arange(1, LC + 1)[:, None, None], 0), axis=0)
    code = jnp.where(q > 0, a_cols * LC + q - 1, -1).T
    p = product(code, a, b)
    return swap_back(p)


def solution(mesh):
    spec = P("rows", "section")
    blocks = P("rows", "section", None, None, None)
    return jax.shard_map(
        on_device, mesh=mesh, in_specs=(blocks, spec, spec, spec), out_specs=blocks, check_vma=False
    )
```

```python
import functools

import jax
import jax.numpy as jnp
from jax import lax
from jax.experimental import pallas as pl
from jax.experimental.pallas import tpu as pltpu
from jax.sharding import PartitionSpec as P

MESH = pl.DeviceIdType.MESH
NX, NY, NZ, NC = 4, 4, 8, 2
RB = 12
GROUPS = 16
BLK = 256
HALF = RB * BLK // 2
META = 16
ROWS = RB * BLK + META
LC = 3


def where_am_i():
    r, s = lax.axis_index("rows"), lax.axis_index("section")
    c = lax.rem(r, 2)
    y = lax.rem(r // 2, NY)
    x = lax.rem(s, 2) * 2 + r // 8
    return x, y, s // 2, c


def device(x, y, z, c):
    return ((lax.rem(x, 2) * NY + y) * 2 + c, z * 2 + x // 2)


def wrap(v, n):
    return lax.rem(v + n, n)


class Copies:
    def __init__(self, send):
        self.send, self.used, self.pending = send, 0, []

    def start(self, cond, src, dst, recv, to):
        copy = pltpu.make_async_remote_copy(
            src_ref=src, dst_ref=dst, send_sem=self.send.at[self.used], recv_sem=recv,
            device_id=to, device_id_type=MESH,
        )
        self.used += 1
        if cond is None:
            copy.start()
        else:
            pl.when(cond)(copy.start)
        self.pending.append((cond, copy))

    def finish(self):
        for cond, copy in self.pending:
            if cond is None:
                copy.wait_send()
            else:
                pl.when(cond)(copy.wait_send)


def enter(partners):
    barrier = pltpu.get_barrier_semaphore()
    for to in partners:
        pl.semaphore_signal(barrier, inc=1, device_id=to, device_id_type=MESH)
    pl.semaphore_wait(barrier, len(partners))


def gather_kernel(x_ref, m_ref, a_ref, b_ref, am_ref, bm_ref, send, recv_a, recv_b, local):
    x, y, z, c = where_am_i()
    h = x // 2
    home = c == h
    away = c != h
    xp, xm = wrap(x + 1, NX), wrap(x - 1, NX)
    yp, ym = wrap(y + 1, NY), wrap(y - 1, NY)
    zp, zm = wrap(z + 1, NZ), wrap(z - 1, NZ)
    sib = device(x, y, z, 1 - c)
    swap = device(wrap(x + 2, NX), y, z, 1 - c)
    to_xp, to_xm = device(xp, y, z, c), device(xm, y, z, c)
    to_yp, to_ym = device(x, yp, z, c), device(x, ym, z, c)
    to_zp, to_zm = device(x, y, zp, c), device(x, y, zm, c)
    enter([sib, swap, to_xp, to_xm, to_yp, to_ym, to_zp, to_zm])
    cp = Copies(send)

    def half(ref, slot, k):
        return ref.at[slot, pl.ds(0, HALF)] if k == 0 else ref.at[slot, pl.ds(HALF, ROWS - HALF)]

    def arrived(cond, ref, recv, slot, part=None):
        view = ref.at[slot] if part is None else half(ref, slot, part)
        sem = recv.at[slot, 0 if part is None else part]
        wait = pltpu.make_async_remote_copy(
            src_ref=view, dst_ref=view, send_sem=send.at[0], recv_sem=sem, device_id=sib, device_id_type=MESH
        ).wait_recv
        if cond is None:
            wait()
        else:
            pl.when(cond)(wait)

    def full(cond, ref, recv, slot, to):
        cp.start(cond, ref.at[slot], ref.at[slot], recv.at[slot, 0], to)

    def part(cond, ref, recv, slot, k, to):
        cp.start(cond, half(ref, slot, k), half(ref, slot, k), recv.at[slot, k], to)

    def group(lo, ys, core):
        return (lo * NY + ys) * 2 + core

    own = group(lax.rem(x, 2), y, c)
    own_sib = group(lax.rem(x, 2), y, 1 - c)
    a_own = 2 * z + c
    body = pl.ds(0, RB * BLK)
    tail = pl.ds(RB * BLK, META)

    mine = [
        pltpu.make_async_copy(x_ref, a_ref.at[a_own, body], local.at[0]),
        pltpu.make_async_copy(m_ref, a_ref.at[a_own, tail], local.at[1]),
        pltpu.make_async_copy(x_ref, b_ref.at[own, body], local.at[2]),
        pltpu.make_async_copy(m_ref, b_ref.at[own, tail], local.at[3]),
    ]

    @pl.when(home)
    def _():
        for m in mine:
            m.start()

    a_partner = 2 * z + (1 - c)
    cp.start(away, x_ref, a_ref.at[a_partner, body], recv_a.at[a_partner, 0], swap)
    cp.start(away, m_ref, a_ref.at[a_partner, tail], recv_a.at[a_partner, 1], swap)
    cp.start(away, x_ref, b_ref.at[own, body], recv_b.at[own, 0], sib)
    cp.start(away, m_ref, b_ref.at[own, tail], recv_b.at[own, 1], sib)

    def z_own(cond):
        full(cond, a_ref, recv_a, a_own, to_zp)
        full(cond, a_ref, recv_a, a_own, to_zm)
        full(cond, a_ref, recv_a, a_own, sib)

    def arrived_in_two(cond, ref, recv, slot):
        for view, k in ((body, 0), (tail, 1)):
            v = ref.at[slot, view]
            wait = pltpu.make_async_remote_copy(
                src_ref=v, dst_ref=v, send_sem=send.at[0], recv_sem=recv.at[slot, k],
                device_id=sib, device_id_type=MESH,
            ).wait_recv
            pl.when(cond)(wait)

    @pl.when(home)
    def _():
        for m in mine:
            m.wait()

    z_own(home)
    arrived_in_two(home, b_ref, recv_b, own_sib)
    here = lax.rem(x, 2)
    mine_x, mine_y = group(here, y, 0), group(here, y, 1)
    for slot, first, second in ((mine_x, (to_xp, to_xm), None), (mine_y, (to_yp, to_ym), None)):
        for to in first:
            full(home, b_ref, recv_b, slot, to)
    for to in (to_yp, to_ym):
        full(home, b_ref, recv_b, mine_x, to)
    for to in (to_xp, to_xm):
        full(home, b_ref, recv_b, mine_y, to)

    arrived_in_two(away, a_ref, recv_a, a_own)
    z_own(away)

    js = [wrap(x - 2 * c - lo, NX) for lo in (0, 1)]

    def y_sends(cond, slot):
        full(cond, b_ref, recv_b, slot, to_yp)
        full(cond, b_ref, recv_b, slot, to_ym)

    def x_sends(cond, slot):
        full(cond, b_ref, recv_b, slot, to_xp)
        full(cond, b_ref, recv_b, slot, to_xm)

    def ring(d):
        for zs, k, to in ((wrap(z - d, NZ), 0, to_zp), (wrap(z + d, NZ), 1, to_zm)):
            slot = 2 * zs + c
            arrived(None, a_ref, recv_a, slot)
            if d < 3:
                full(None, a_ref, recv_a, slot, to)
            else:
                part(None, a_ref, recv_a, slot, k, to)
            full(None, a_ref, recv_a, slot, sib)

    def x_pass(lo, slot):
        j = js[lo]
        for jj, k, to in ((1, 0, to_xp), (3, 1, to_xm)):
            arrived(j == jj, b_ref, recv_b, slot)
            part(j == jj, b_ref, recv_b, slot, k, to)

    for lo in (0, 1):
        slot = group(lo, y, 0)
        x_pass(lo, slot)
        y_sends((js[lo] == 1) | (js[lo] == 3), slot)
    for ys, k, to in ((ym, 0, to_yp), (yp, 1, to_ym)):
        slot = group(here, ys, 1)
        arrived(home, b_ref, recv_b, slot)
        part(home, b_ref, recv_b, slot, k, to)
        x_sends(home, slot)
    ring(1)
    for lo in (0, 1):
        slot = group(lo, y, 0)
        for k in (0, 1):
            arrived(js[lo] == 2, b_ref, recv_b, slot, k)
        y_sends(js[lo] == 2, slot)
    y2 = wrap(y + 2, NY)
    slot = group(here, y2, 1)
    for k in (0, 1):
        arrived(home, b_ref, recv_b, slot, k)
    x_sends(home, slot)
    ring(2)
    for lo in (0, 1):
        for ys, k, to in ((ym, 0, to_yp), (yp, 1, to_ym)):
            slot = group(lo, ys, 0)
            arrived(None, b_ref, recv_b, slot)
            part(None, b_ref, recv_b, slot, k, to)
        x_pass(lo, group(lo, y, 1))
        for ys in (ym, yp):
            x_pass(lo, group(lo, ys, 1))
    ring(3)
    for lo in (0, 1):
        x_pass(lo, group(lo, y2, 1))
    for lo in (0, 1):
        for k in (0, 1):
            arrived(None, b_ref, recv_b, group(lo, y2, 0), k)
            for ys in (y, ym, yp, y2):
                arrived(js[lo] == 2, b_ref, recv_b, group(lo, ys, 1), k)
    slot = 2 * wrap(z + 4, NZ) + c
    for k in (0, 1):
        arrived(None, a_ref, recv_a, slot, k)
        part(None, a_ref, recv_a, slot, k, sib)
    for d in range(NZ):
        slot = 2 * wrap(z + d, NZ) + 1 - c
        if d == 4:
            for k in (0, 1):
                arrived(None, a_ref, recv_a, slot, k)
        else:
            arrived(None, a_ref, recv_a, slot)
    tails = [
        pltpu.make_async_copy(a_ref.at[:, tail], am_ref, local.at[0]),
        pltpu.make_async_copy(b_ref.at[:, tail], bm_ref, local.at[1]),
    ]
    for t in tails:
        t.start()
    for t in tails:
        t.wait()
    cp.finish()


def gather(x, meta):
    shape = jax.ShapeDtypeStruct((GROUPS, ROWS, 128), jnp.bfloat16)
    tails = jax.ShapeDtypeStruct((GROUPS, META, 128), jnp.bfloat16)
    return pl.pallas_call(
        gather_kernel,
        out_shape=(shape, shape, tails, tails),
        in_specs=[pl.BlockSpec(memory_space=pltpu.VMEM)] * 2,
        out_specs=(pl.BlockSpec(memory_space=pl.ANY),) * 4,
        scratch_shapes=[
            pltpu.SemaphoreType.DMA((96,)),
            pltpu.SemaphoreType.DMA((GROUPS, 2)),
            pltpu.SemaphoreType.DMA((GROUPS, 2)),
            pltpu.SemaphoreType.DMA((4,)),
        ],
        compiler_params=pltpu.CompilerParams(collective_id=0, has_side_effects=True),
        name="gather_strip_and_panel",
    )(x, meta)


def product_kernel(slot_ref, a_ref, b_ref, o_ref, acc):
    i = pl.program_id(0)
    for q in range(LC):
        acc[q] = jnp.zeros_like(acc[q])

    @pl.loop(0, GROUPS)
    def _(t):
        code = slot_ref[i, t]

        @pl.when(code >= 0)
        def _():
            m = code // LC
            q = code - m * LC
            a_re, a_im = a_ref[t, :128, :], a_ref[t, 128:, :]
            row = pl.multiple_of(m * BLK, BLK)
            b = b_ref[t, pl.ds(row, BLK), :]
            b_re, b_im = b[:128], b[128:]
            lhs = jnp.concatenate([a_re, a_im], axis=1)
            rhs = jnp.concatenate(
                [jnp.concatenate([b_re, b_im], axis=1), jnp.concatenate([-b_im, b_re], axis=1)], axis=0
            )
            acc[q] += jnp.dot(lhs, rhs, preferred_element_type=jnp.float32)

    for q in range(LC):
        o_ref[0, q, 0] = acc[q][:, :128].astype(jnp.bfloat16)
        o_ref[0, q, 1] = acc[q][:, 128:].astype(jnp.bfloat16)


def product(code, a, b):
    return pl.pallas_call(
        product_kernel,
        out_shape=jax.ShapeDtypeStruct((RB, LC, 2, 128, 128), jnp.bfloat16),
        grid_spec=pltpu.PrefetchScalarGridSpec(
            num_scalar_prefetch=1,
            grid=(RB,),
            in_specs=[
                pl.BlockSpec((GROUPS, BLK, 128), lambda i, code: (0, i, 0)),
                pl.BlockSpec((GROUPS, ROWS, 128), lambda i, code: (0, 0, 0), pipeline_mode=pl.Buffered(1)),
            ],
            out_specs=pl.BlockSpec((1, LC, 2, 128, 128), lambda i, code: (i, 0, 0, 0, 0)),
            scratch_shapes=[pltpu.VMEM((LC, 128, 256), jnp.float32)],
        ),
        compiler_params=pltpu.CompilerParams(
            dimension_semantics=("arbitrary",), vmem_limit_bytes=32 << 20
        ),
        name="matched_block_products",
    )(code, a, b)


def swap_kernel(p_ref, o_ref, send, recv, local):
    x, y, z, c = where_am_i()
    home = c == x // 2
    away = c != x // 2
    to = device(wrap(x + 2, NX), y, z, 1 - c)
    enter([to])
    keep = pltpu.make_async_copy(p_ref, o_ref, local.at[0])
    move = pltpu.make_async_remote_copy(
        src_ref=p_ref, dst_ref=o_ref, send_sem=send, recv_sem=recv, device_id=to, device_id_type=MESH
    )
    pl.when(home)(keep.start)
    pl.when(away)(move.start)
    pl.when(home)(keep.wait)
    pl.when(away)(move.wait)


def swap_back(p):
    return pl.pallas_call(
        swap_kernel,
        out_shape=jax.ShapeDtypeStruct(p.shape, p.dtype),
        in_specs=[pl.BlockSpec(memory_space=pltpu.VMEM)],
        out_specs=pl.BlockSpec(memory_space=pl.ANY),
        scratch_shapes=[pltpu.SemaphoreType.DMA, pltpu.SemaphoreType.DMA, pltpu.SemaphoreType.DMA((1,))],
        compiler_params=pltpu.CompilerParams(collective_id=1, has_side_effects=True),
        name="swap_results",
    )(p)


def on_device(x_blocks, x_cols, c_cols, c_keep):
    x = x_blocks.reshape(RB * BLK, 128)
    wanted = jnp.where(c_keep != 0, c_cols, -2)
    meta = jnp.concatenate([x_cols.T, wanted.T], axis=0)
    meta = jnp.pad(meta, ((0, META - 1 - LC), (0, 128 - RB))).astype(jnp.bfloat16)
    a, b, a_meta, b_meta = gather(x, meta)
    a_meta = a_meta[:, :, :RB].astype(jnp.int32)
    b_meta = b_meta[:, :, :RB].astype(jnp.int32)
    a_cols = a_meta[:, 0]
    pick = a_cols[:, :, None] == jnp.arange(RB)[None, None, :]
    column = jnp.sum(jnp.where(pick, b_meta[:, 0][:, None, :] + 1, 0), axis=2) - 1
    mine = lax.dynamic_index_in_dim(a_meta, lax.axis_index("section") // 2 * 2 + lax.rem(lax.axis_index("rows"), 2), 0, False)
    hit = (column[None] == mine[1 : 1 + LC][:, None, :]) & (column >= 0)[None]
    q = jnp.sum(jnp.where(hit, jnp.arange(1, LC + 1)[:, None, None], 0), axis=0)
    code = jnp.where(q > 0, a_cols * LC + q - 1, -1).T
    p = product(code, a, b)
    return swap_back(p)


def solution(mesh):
    spec = P("rows", "section")
    blocks = P("rows", "section", None, None, None)
    return jax.shard_map(
        on_device, mesh=mesh, in_specs=(blocks, spec, spec, spec), out_specs=blocks, check_vma=False
    )
```

```python
import jax
import jax.numpy as jnp
from jax import lax
from jax.experimental import pallas as pl
from jax.experimental.pallas import tpu as pltpu
from jax.sharding import PartitionSpec as P

MESH = pl.DeviceIdType.MESH
NX, NY, NZ, NC = 4, 4, 8, 2
RB = 12
GROUPS = 16
BLK = 256
HALF = RB // 2
META = 8
LC = 3
SLOTS = 16


def where_am_i():
    r, s = lax.axis_index("rows"), lax.axis_index("section")
    c = lax.rem(r, 2)
    y = lax.rem(r // 2, NY)
    x = lax.rem(s, 2) * 2 + r // 8
    return x, y, s // 2, c


def device(x, y, z, c):
    return ((lax.rem(x, 2) * NY + y) * 2 + c, z * 2 + x // 2)


def wrap(v, n):
    return lax.rem(v + n, n)


class Copies:
    def __init__(self, send):
        self.send, self.used, self.pending = send, 0, []

    def start(self, cond, src, dst, recv, to):
        copy = pltpu.make_async_remote_copy(
            src_ref=src, dst_ref=dst, send_sem=self.send.at[self.used], recv_sem=recv,
            device_id=to, device_id_type=MESH,
        )
        self.used += 1
        if cond is None:
            copy.start()
        else:
            pl.when(cond)(copy.start)
        self.pending.append((cond, copy))

    def finish(self):
        for cond, copy in self.pending:
            if cond is None:
                copy.wait_send()
            else:
                pl.when(cond)(copy.wait_send)


def enter(partners):
    barrier = pltpu.get_barrier_semaphore()
    for to in partners:
        pl.semaphore_signal(barrier, inc=1, device_id=to, device_id_type=MESH)
    pl.semaphore_wait(barrier, len(partners))


def square_kernel(
    x_ref, m_ref, o_ref, a_ref, b_ref, am_ref, bm_ref, c_ref, tab_v, tab_s,
    send, recv_a, recv_b, recv_m, send_c, recv_c, local,
):
    x, y, z, c = where_am_i()
    h = x // 2
    home = c == h
    away = c != h
    xp, xm = wrap(x + 1, NX), wrap(x - 1, NX)
    yp, ym = wrap(y + 1, NY), wrap(y - 1, NY)
    zp, zm = wrap(z + 1, NZ), wrap(z - 1, NZ)
    sib = device(x, y, z, 1 - c)
    swap = device(wrap(x + 2, NX), y, z, 1 - c)
    to_xp, to_xm = device(xp, y, z, c), device(xm, y, z, c)
    to_yp, to_ym = device(x, yp, z, c), device(x, ym, z, c)
    to_zp, to_zm = device(x, y, zp, c), device(x, y, zm, c)
    enter([sib, swap, to_xp, to_xm, to_yp, to_ym, to_zp, to_zm])
    cp = Copies(send)
    strip = (a_ref, am_ref, recv_a, 0)
    panel = (b_ref, bm_ref, recv_b, 1)

    def half(ref, slot, k):
        return ref.at[slot, pl.ds(k * HALF, HALF)]

    def wait_for(cond, view, sem):
        wait = pltpu.make_async_remote_copy(
            src_ref=view, dst_ref=view, send_sem=send.at[0], recv_sem=sem, device_id=sib, device_id_type=MESH
        ).wait_recv
        if cond is None:
            wait()
        else:
            pl.when(cond)(wait)

    def arrived(cond, kind, slot, part=None):
        ref, meta, recv, k = kind
        view = ref.at[slot] if part is None else half(ref, slot, part)
        wait_for(cond, view, recv.at[slot, part or 0])
        if part != 1:
            wait_for(cond, meta.at[slot], recv_m.at[k, slot])

    def full(cond, kind, slot, to):
        ref, meta, recv, k = kind
        cp.start(cond, meta.at[slot], meta.at[slot], recv_m.at[k, slot], to)
        cp.start(cond, ref.at[slot], ref.at[slot], recv.at[slot, 0], to)

    def part(cond, kind, slot, p, to):
        ref, meta, recv, k = kind
        if p == 0:
            cp.start(cond, meta.at[slot], meta.at[slot], recv_m.at[k, slot], to)
        cp.start(cond, half(ref, slot, p), half(ref, slot, p), recv.at[slot, p], to)

    def group(lo, ys, core):
        return (lo * NY + ys) * 2 + core

    here = lax.rem(x, 2)
    own = group(here, y, c)
    a_own = 2 * z + c
    a_partner = 2 * z + (1 - c)

    def give(kind, slot, to):
        ref, meta, recv, k = kind
        cp.start(away, m_ref, meta.at[slot], recv_m.at[k, slot], to)
        cp.start(away, x_ref, ref.at[slot], recv.at[slot, 0], to)

    give(strip, a_partner, swap)
    give(panel, own, sib)

    def keep(kind, slot):
        ref, meta, recv, k = kind
        ref[slot] = x_ref[...]
        meta[slot] = m_ref[...]

    @pl.when(home)
    def _():
        keep(strip, a_own)
        keep(panel, own)

    def z_own(cond):
        for to in (to_zp, to_zm, sib):
            full(cond, strip, a_own, to)

    z_own(home)
    arrived(home, panel, group(here, y, 1 - c))
    mine_x, mine_y = group(here, y, 0), group(here, y, 1)
    for to in (to_xp, to_xm):
        full(home, panel, mine_x, to)
    for to in (to_yp, to_ym):
        full(home, panel, mine_y, to)
    for to in (to_yp, to_ym):
        full(home, panel, mine_x, to)
    for to in (to_xp, to_xm):
        full(home, panel, mine_y, to)
    arrived(away, strip, a_own)
    z_own(away)

    js = [wrap(x - 2 * c - lo, NX) for lo in (0, 1)]

    def y_sends(cond, slot):
        full(cond, panel, slot, to_yp)
        full(cond, panel, slot, to_ym)

    def x_sends(cond, slot):
        full(cond, panel, slot, to_xp)
        full(cond, panel, slot, to_xm)

    def ring(d):
        for zs, k, to in ((wrap(z - d, NZ), 0, to_zp), (wrap(z + d, NZ), 1, to_zm)):
            slot = 2 * zs + c
            arrived(None, strip, slot)
            if d < 3:
                full(None, strip, slot, to)
            else:
                part(None, strip, slot, k, to)
            full(None, strip, slot, sib)

    def x_pass(lo, slot):
        j = js[lo]
        for jj, k, to in ((1, 0, to_xp), (3, 1, to_xm)):
            arrived(j == jj, panel, slot)
            part(j == jj, panel, slot, k, to)

    for lo in (0, 1):
        slot = group(lo, y, 0)
        x_pass(lo, slot)
        y_sends((js[lo] == 1) | (js[lo] == 3), slot)
    for ys, k, to in ((ym, 0, to_yp), (yp, 1, to_ym)):
        slot = group(here, ys, 1)
        arrived(home, panel, slot)
        part(home, panel, slot, k, to)
        x_sends(home, slot)
    ring(1)
    for lo in (0, 1):
        slot = group(lo, y, 0)
        for k in (0, 1):
            arrived(js[lo] == 2, panel, slot, k)
        y_sends(js[lo] == 2, slot)
    y2 = wrap(y + 2, NY)
    slot = group(here, y2, 1)
    for k in (0, 1):
        arrived(home, panel, slot, k)
    x_sends(home, slot)
    ring(2)
    for lo in (0, 1):
        for ys, k, to in ((ym, 0, to_yp), (yp, 1, to_ym)):
            slot = group(lo, ys, 0)
            arrived(None, panel, slot)
            part(None, panel, slot, k, to)
        x_pass(lo, group(lo, y, 1))
        for ys in (ym, yp):
            x_pass(lo, group(lo, ys, 1))
    ring(3)
    for lo in (0, 1):
        x_pass(lo, group(lo, y2, 1))
    for lo in (0, 1):
        for k in (0, 1):
            arrived(None, panel, group(lo, y2, 0), k)
            for ys in (y, ym, yp, y2):
                arrived(js[lo] == 2, panel, group(lo, ys, 1), k)
    slot = 2 * wrap(z + 4, NZ) + c
    for k in (0, 1):
        arrived(None, strip, slot, k)
        part(None, strip, slot, k, sib)
    for d in range(NZ):
        slot = 2 * wrap(z + d, NZ) + 1 - c
        if d == 4:
            for k in (0, 1):
                arrived(None, strip, slot, k)
        else:
            arrived(None, strip, slot)

    sub = lax.broadcasted_iota(jnp.int32, (SLOTS, 128), 0)
    lane = lax.broadcasted_iota(jnp.int32, (SLOTS, 128), 1)

    def upright(row):
        return jnp.sum(jnp.where(lane == sub, row, 0), axis=1, keepdims=True)

    wanted = [upright(am_ref[a_own, pl.ds(1 + q, 1), :]) for q in range(LC)]
    blocks = codes = jnp.zeros((SLOTS, 128), jnp.int32)
    for t in range(GROUPS):
        col = upright(am_ref[t, pl.ds(0, 1), :])
        far = jnp.sum(jnp.where(lane == col, bm_ref[t, pl.ds(0, 1), :] + 1, 0), axis=1, keepdims=True) - 1
        code = jnp.zeros_like(col)
        for q in range(LC):
            code = code + jnp.where((col >= 0) & (far >= 0) & (far == wanted[q]), q + 1, 0)
        blocks = jnp.where(lane == t, jnp.maximum(col, 0), blocks)
        codes = jnp.where(lane == t, code, codes)
    tab_v[0] = blocks
    tab_v[1] = codes
    to_smem = pltpu.make_async_copy(tab_v.at[0], tab_s, local.at[0])
    to_smem.start()
    to_smem.wait()

    def moved(i):
        return pltpu.make_async_remote_copy(
            src_ref=c_ref.at[i], dst_ref=o_ref.at[i], send_sem=send_c.at[i], recv_sem=recv_c.at[i],
            device_id=swap, device_id_type=MESH,
        )

    def stored(i):
        return pltpu.make_async_copy(c_ref.at[i], o_ref.at[i], send_c.at[i])

    @pl.loop(0, RB)
    def _(i):
        row_codes = tab_v[1, pl.ds(i, 1), :]
        masks = [jnp.where(row_codes == k + 1, 1.0, 0.0).astype(jnp.bfloat16) for k in range(LC)]
        total = None
        for t in range(GROUPS):
            a = a_ref[t, i]
            lhs = jnp.concatenate([a[:128], a[128:]], axis=1)
            lhs = jnp.concatenate([lhs * masks[k][:, t : t + 1] for k in range(LC)], axis=0)
            b = b_ref[t, tab_s[i, t]]
            rhs = jnp.concatenate(
                [jnp.concatenate([b[:128], b[128:]], axis=1), jnp.concatenate([-b[128:], b[:128]], axis=1)], axis=0
            )
            term = jnp.dot(lhs, rhs, preferred_element_type=jnp.float32)
            total = term if total is None else total + term
        for k in range(LC):
            for part_of in (0, 1):
                c_ref[i, k, part_of] = total[128 * k : 128 * (k + 1), 128 * part_of : 128 * (part_of + 1)].astype(
                    jnp.bfloat16
                )

        @pl.when(away)
        def _():
            moved(i).start()

        @pl.when(home)
        def _():
            stored(i).start()

    @pl.loop(0, RB)
    def _(i):
        @pl.when(away)
        def _():
            moved(i).wait()

        @pl.when(home)
        def _():
            stored(i).wait()

    cp.finish()


def square(x, meta):
    dma = pltpu.SemaphoreType.DMA
    return pl.pallas_call(
        square_kernel,
        out_shape=jax.ShapeDtypeStruct((RB, LC, 2, 128, 128), jnp.bfloat16),
        in_specs=[pl.BlockSpec(memory_space=pltpu.VMEM)] * 2,
        out_specs=pl.BlockSpec(memory_space=pl.ANY),
        scratch_shapes=[
            pltpu.VMEM((GROUPS, RB, BLK, 128), jnp.bfloat16),
            pltpu.VMEM((GROUPS, RB, BLK, 128), jnp.bfloat16),
            pltpu.VMEM((GROUPS, META, 128), jnp.int32),
            pltpu.VMEM((GROUPS, META, 128), jnp.int32),
            pltpu.VMEM((RB, LC, 2, 128, 128), jnp.bfloat16),
            pltpu.VMEM((2, SLOTS, 128), jnp.int32),
            pltpu.SMEM((SLOTS, 128), jnp.int32),
            dma((128,)),
            dma((GROUPS, 2)),
            dma((GROUPS, 2)),
            dma((2, GROUPS)),
            dma((RB,)),
            dma((RB,)),
            dma((1,)),
        ],
        compiler_params=pltpu.CompilerParams(
            collective_id=0, has_side_effects=True, vmem_limit_bytes=48 << 20
        ),
        name="gather_and_square",
    )(x, meta)


def on_device(x_blocks, x_cols, c_cols, c_keep):
    x = x_blocks.reshape(RB, BLK, 128)
    wanted = jnp.where(c_keep != 0, c_cols, -2)
    meta = jnp.concatenate([x_cols.T, wanted.T], axis=0)
    meta = jnp.pad(meta, ((0, META - 1 - LC), (0, 128 - RB)), constant_values=-1)
    return square(x, meta)


def solution(mesh):
    spec = P("rows", "section")
    blocks = P("rows", "section", None, None, None)
    return jax.shard_map(
        on_device, mesh=mesh, in_specs=(blocks, spec, spec, spec), out_specs=blocks, check_vma=False
    )
```

```python
import jax
import jax.numpy as jnp
from jax import lax
from jax.experimental import pallas as pl
from jax.experimental.pallas import tpu as pltpu
from jax.sharding import PartitionSpec as P

MESH = pl.DeviceIdType.MESH
NX, NY, NZ, NC = 4, 4, 8, 2
RB = 12
GROUPS = 16
BLK = 256
HALF = RB // 2
META = 8
LC = 3
SLOTS = 16
SENDS = 194


def where_am_i():
    r, s = lax.axis_index("rows"), lax.axis_index("section")
    c = lax.rem(r, 2)
    y = lax.rem(r // 2, NY)
    x = lax.rem(s, 2) * 2 + r // 8
    return x, y, s // 2, c


def device(x, y, z, c):
    return ((lax.rem(x, 2) * NY + y) * 2 + c, z * 2 + x // 2)


def wrap(v, n):
    return lax.rem(v + n, n)


class Copies:
    def __init__(self, send):
        self.send, self.used, self.pending = send, 0, []

    def start(self, cond, src, dst, recv, to):
        copy = pltpu.make_async_remote_copy(
            src_ref=src, dst_ref=dst, send_sem=self.send.at[self.used], recv_sem=recv,
            device_id=to, device_id_type=MESH,
        )
        self.used += 1
        if cond is None:
            copy.start()
        else:
            pl.when(cond)(copy.start)
        self.pending.append((cond, copy))

    def finish(self):
        for cond, copy in self.pending:
            if cond is None:
                copy.wait_send()
            else:
                pl.when(cond)(copy.wait_send)


def enter(partners):
    barrier = pltpu.get_barrier_semaphore()
    for to in partners:
        pl.semaphore_signal(barrier, inc=1, device_id=to, device_id_type=MESH)
    pl.semaphore_wait(barrier, len(partners))


def square_kernel(
    x_ref, xc_ref, cc_ref, ck_ref, o_ref, a_ref, b_ref, am_ref, bm_ref, m_ref, c_ref, tab_v, tab_s,
    send, recv_a, recv_b, recv_m, send_c, recv_c, local,
):
    x, y, z, c = where_am_i()
    h = x // 2
    home = c == h
    away = c != h
    xp, xm = wrap(x + 1, NX), wrap(x - 1, NX)
    yp, ym, y2 = wrap(y + 1, NY), wrap(y - 1, NY), wrap(y + 2, NY)
    zp, zm = wrap(z + 1, NZ), wrap(z - 1, NZ)
    sib = device(x, y, z, 1 - c)
    swap = device(wrap(x + 2, NX), y, z, 1 - c)
    to_xp, to_xm = device(xp, y, z, c), device(xm, y, z, c)
    to_yp, to_ym = device(x, yp, z, c), device(x, ym, z, c)
    to_zp, to_zm = device(x, y, zp, c), device(x, y, zm, c)
    here = lax.rem(x, 2)

    def group(lo, ys, core):
        return (lo * NY + ys) * 2 + core

    own = group(here, y, c)
    a_own = 2 * z + c
    a_partner = 2 * z + (1 - c)

    mine = [
        pltpu.make_async_copy(x_ref, a_ref.at[a_own], local.at[0]),
        pltpu.make_async_copy(x_ref, b_ref.at[own], local.at[1]),
    ]

    @pl.when(home)
    def _():
        for copy in mine:
            copy.start()

    m_ref[...] = jnp.full((META, 128), -1, jnp.int32)
    m_ref[0:1, 0:RB] = xc_ref[...]
    m_ref[1 : 1 + LC, 0:RB] = jnp.where(ck_ref[...] != 0, cc_ref[...], -2)

    @pl.when(home)
    def _():
        am_ref[a_own] = m_ref[...]
        bm_ref[own] = m_ref[...]

    enter([sib, swap, device(wrap(x + 2, NX), y, z, c), to_xp, to_xm, to_yp, to_ym, to_zp, to_zm])
    cp = Copies(send)

    def wait_for(cond, view, sem):
        wait = pltpu.make_async_remote_copy(
            src_ref=view, dst_ref=view, send_sem=send.at[0], recv_sem=sem, device_id=sib, device_id_type=MESH
        ).wait_recv
        if cond is None:
            wait()
        else:
            pl.when(cond)(wait)

    def a_view(slot, core, k):
        rows = HALF if k is None else HALF // 2
        return a_ref.at[slot, pl.ds(core * HALF + (k or 0) * rows, rows)]

    def a_send(cond, slot, to, k=None):
        if k != 1:
            cp.start(cond, am_ref.at[slot], am_ref.at[slot], recv_m.at[0, slot], to)
        cp.start(cond, a_view(slot, c, k), a_view(slot, c, k), recv_a.at[slot, k or 0], to)

    def a_sib(cond, slot, k=None):
        cp.start(cond, a_view(slot, c, k), a_view(slot, c, k), recv_a.at[slot, 2 + (k or 0)], sib)

    def a_wait(cond, slot, k=None):
        wait_for(cond, a_view(slot, c, k), recv_a.at[slot, k or 0])
        if k != 1:
            wait_for(cond, am_ref.at[slot], recv_m.at[0, slot])

    def a_wait_sib(cond, slot, k=None):
        wait_for(cond, a_view(slot, 1 - c, k), recv_a.at[slot, 2 + (k or 0)])

    def b_view(slot, unit, k):
        _, first, rows, _ = unit
        if k is not None:
            rows = rows // 2
            first = first + k * rows
        return b_ref.at[slot, pl.ds(first, rows)]

    def b_send(cond, slot, unit, to, k=None):
        if k != 1 and unit[3] == 0:
            cp.start(cond, bm_ref.at[slot], bm_ref.at[slot], recv_m.at[1, slot], to)
        cp.start(cond, b_view(slot, unit, k), b_view(slot, unit, k), recv_b.at[slot, unit[3], k or 0], to)

    def b_wait(cond, slot, unit, k=None):
        wait_for(cond, b_view(slot, unit, k), recv_b.at[slot, unit[3], k or 0])
        if k != 1 and unit[3] == 0:
            wait_for(cond, bm_ref.at[slot], recv_m.at[1, slot])

    x_first = [(0, 0, RB, 0), (1, 0, 2, 0)]
    y_first = (1, 2, RB - 2, 1)

    for core in (0, 1):
        to = device(wrap(x + 2, NX), y, z, core)
        cp.start(away, m_ref, am_ref.at[a_partner], recv_m.at[0, a_partner], to)
        cp.start(away, x_ref.at[pl.ds(core * HALF, HALF)], a_view(a_partner, core, None), recv_a.at[a_partner, 0], to)
    cp.start(away, m_ref, bm_ref.at[own], recv_m.at[1, own], sib)
    cp.start(away, x_ref, b_ref.at[own], recv_b.at[own, 0, 0], sib)

    @pl.when(home)
    def _():
        for copy in mine:
            copy.wait()

    def z_own(cond, slot):
        for to in (to_zp, to_zm):
            a_send(cond, slot, to)

    a_first, a_swapped = 2 * z + h, 2 * z + 1 - h
    cp.start(home, am_ref.at[a_first], am_ref.at[a_first], recv_m.at[0, a_first], sib)
    cp.start(home, a_view(a_first, 1 - c, None), a_view(a_first, 1 - c, None), recv_a.at[a_first, 0], sib)
    z_own(home, a_first)
    a_sib(home, a_first)
    a_wait(away, a_first)
    z_own(away, a_first)
    from_sib = group(here, y, 1 - c)
    wait_for(home, b_ref.at[from_sib], recv_b.at[from_sib, 0, 0])
    wait_for(home, bm_ref.at[from_sib], recv_m.at[1, from_sib])

    def x_sends(cond, slot, unit):
        for to in (to_xp, to_xm):
            b_send(cond, slot, unit, to)

    def y_sends(cond, slot, unit):
        for to in (to_yp, to_ym):
            b_send(cond, slot, unit, to)

    js = [wrap(x - 2 * c - lo, NX) for lo in (0, 1)]
    beside = [(j == 1) | (j == 3) for j in js]

    def x_pass(cond, lo, ys, unit):
        slot = group(lo, ys, unit[0])
        for jj, k, to in ((1, 0, to_xp), (3, 1, to_xm)):
            on = cond & (js[lo] == jj)
            b_wait(on, slot, unit)
            b_send(on, slot, unit, to, k)

    def x_end(lo, ys, unit):
        for k in (0, 1):
            b_wait(js[lo] == 2, group(lo, ys, unit[0]), unit, k)

    def y_pass(cond, lo, unit):
        for ys, k, to in ((ym, 0, to_yp), (yp, 1, to_ym)):
            slot = group(lo, ys, unit[0])
            b_wait(cond, slot, unit)
            b_send(cond, slot, unit, to, k)

    def y_end(cond, lo, unit):
        for k in (0, 1):
            b_wait(cond, group(lo, y2, unit[0]), unit, k)

    def ring(d):
        for par in (h, 1 - h):
            for zs, k, to in ((wrap(z - d, NZ), 0, to_zp), (wrap(z + d, NZ), 1, to_zm)):
                slot = 2 * zs + par
                a_wait(None, slot)
                a_send(None, slot, to, k if d == 3 else None)
                a_sib(None, slot)

    x_sends(home, group(here, y, 0), x_first[0])
    y_sends(home, group(here, y, 1), y_first)
    x_sends(home, group(here, y, 1), x_first[1])
    y_sends(home, group(here, y, 0), x_first[0])
    y_sends(home, group(here, y, 1), x_first[1])
    x_sends(home, group(here, y, 1), y_first)

    a_wait(None, a_swapped)
    z_own(None, a_swapped)
    a_sib(None, a_swapped)
    for lo in (0, 1):
        x_pass(True, lo, y, x_first[0])
        y_sends(away & beside[lo], group(lo, y, 0), x_first[0])
    for lo in (0, 1):
        x_pass(True, lo, y, x_first[1])
        y_sends(away & beside[lo], group(lo, y, 1), x_first[1])
    y_pass(home, here, y_first)
    for ys in (ym, yp):
        x_sends(home, group(here, ys, 1), y_first)
    ring(1)
    for lo in (0, 1):
        x_end(lo, y, x_first[0])
        y_sends(js[lo] == 2, group(lo, y, 0), x_first[0])
    for lo in (0, 1):
        x_end(lo, y, x_first[1])
        y_sends(js[lo] == 2, group(lo, y, 1), x_first[1])
    y_end(home, here, y_first)
    x_sends(home, group(here, y2, 1), y_first)
    ring(2)
    for lo in (0, 1):
        y_pass(away, lo, x_first[0])
    for lo in (0, 1):
        y_pass(away, lo, x_first[1])
    for unit in x_first:
        y_pass(home, here, unit)
    for lo in (0, 1):
        x_pass(True, lo, y, y_first)
    for unit in x_first:
        for lo in (0, 1):
            y_sends(home & beside[lo], group(lo, y, unit[0]), unit)
    for lo in (0, 1):
        x_pass(True, lo, ym, y_first)
    for lo in (0, 1):
        x_pass(True, lo, yp, y_first)
    ring(3)
    for lo in (0, 1):
        x_pass(True, lo, y2, y_first)
    for unit in x_first:
        for lo in (0, 1):
            y_end(away, lo, unit)
    for ys in (y, ym, yp, y2):
        for lo in (0, 1):
            x_end(lo, ys, y_first)
    for unit in x_first:
        for lo in (0, 1):
            y_pass(home & beside[lo], lo, unit)

    for par in (h, 1 - h):
        slot = 2 * wrap(z + 4, NZ) + par
        for k in (0, 1):
            a_wait(None, slot, k)
            a_sib(None, slot, k)
    a_wait_sib(away, a_first)
    a_wait_sib(None, a_swapped)
    for d in range(1, NZ):
        for par in (h, 1 - h):
            for k in (0, 1) if d == 4 else (None,):
                a_wait_sib(None, 2 * wrap(z + d, NZ) + par, k)

    for unit in x_first:
        for lo in (0, 1):
            y_end(home, lo, unit)

    order = [group(lo, ys, core) for ys in (y, ym, yp, y2) for lo in (0, 1) for core in (0, 1)]
    sub = lax.broadcasted_iota(jnp.int32, (SLOTS, 128), 0)
    lane = lax.broadcasted_iota(jnp.int32, (SLOTS, 128), 1)

    def upright(row):
        return jnp.sum(jnp.where(lane == sub, row, 0), axis=1, keepdims=True)

    def look_up(places):
        wanted = [upright(am_ref[a_own, pl.ds(1 + q, 1), :]) for q in range(LC)]
        blocks = codes = jnp.zeros((SLOTS, 128), jnp.int32)
        for p in places:
            t = order[p]
            col = upright(am_ref[t, pl.ds(0, 1), :])
            far = jnp.sum(jnp.where(lane == col, bm_ref[t, pl.ds(0, 1), :] + 1, 0), axis=1, keepdims=True) - 1
            code = jnp.zeros_like(col)
            for q in range(LC):
                code = code + jnp.where((col >= 0) & (far >= 0) & (far == wanted[q]), q + 1, 0)
            blocks = jnp.where(lane == p, jnp.maximum(col, 0), blocks)
            codes = jnp.where(lane == p, code, codes)
        tab_v[0] = blocks
        tab_v[1] = codes
        to_smem = pltpu.make_async_copy(tab_v.at[0], tab_s, local.at[2])
        to_smem.start()
        to_smem.wait()

    def multiply(i, places, total):
        row_codes = tab_v[1, pl.ds(i, 1), :]
        masks = [jnp.where(row_codes == k + 1, 1.0, 0.0).astype(jnp.bfloat16) for k in range(LC)]
        for p in places:
            t = order[p]
            a = a_ref[t, i]
            lhs = jnp.concatenate([a[:128], a[128:]], axis=1)
            lhs = jnp.concatenate([lhs * masks[k][:, p : p + 1] for k in range(LC)], axis=0)
            b = b_ref[t, tab_s[i, p]]
            rhs = jnp.concatenate(
                [jnp.concatenate([b[:128], b[128:]], axis=1), jnp.concatenate([-b[128:], b[:128]], axis=1)], axis=0
            )
            term = jnp.dot(lhs, rhs, preferred_element_type=jnp.float32)
            total = term if total is None else total + term
        return total

    def finish_row(i, total):
        for k in range(LC):
            for p in (0, 1):
                c_ref[i, k, p] = total[128 * k : 128 * (k + 1), 128 * p : 128 * (p + 1)].astype(jnp.bfloat16)

    def moved(i):
        return pltpu.make_async_remote_copy(
            src_ref=c_ref.at[i], dst_ref=o_ref.at[i], send_sem=send_c.at[i], recv_sem=recv_c.at[i],
            device_id=swap, device_id_type=MESH,
        )

    def stored(i):
        return pltpu.make_async_copy(c_ref.at[i], o_ref.at[i], send_c.at[i])

    look_up(range(GROUPS))

    @pl.loop(0, RB)
    def _(i):
        finish_row(i, multiply(i, range(GROUPS), None))

        @pl.when(away)
        def _():
            moved(i).start()

        @pl.when(home)
        def _():
            stored(i).start()

    @pl.loop(0, RB)
    def _(i):
        @pl.when(away)
        def _():
            moved(i).wait()

        @pl.when(home)
        def _():
            stored(i).wait()

    cp.finish()


def square(x, x_cols, c_cols, c_keep):
    dma = pltpu.SemaphoreType.DMA
    vmem = pltpu.VMEM
    return pl.pallas_call(
        square_kernel,
        out_shape=jax.ShapeDtypeStruct((RB, LC, 2, 128, 128), jnp.bfloat16),
        in_specs=[pl.BlockSpec(memory_space=pltpu.HBM)] + [pl.BlockSpec(memory_space=vmem)] * 3,
        out_specs=pl.BlockSpec(memory_space=pl.ANY),
        scratch_shapes=[
            vmem((GROUPS, RB, BLK, 128), jnp.bfloat16),
            vmem((GROUPS, RB, BLK, 128), jnp.bfloat16),
            vmem((GROUPS, META, 128), jnp.int32),
            vmem((GROUPS, META, 128), jnp.int32),
            vmem((META, 128), jnp.int32),
            vmem((RB, LC, 2, 128, 128), jnp.bfloat16),
            vmem((2, SLOTS, 128), jnp.int32),
            pltpu.SMEM((SLOTS, 128), jnp.int32),
            dma((SENDS,)),
            dma((GROUPS, 4)),
            dma((GROUPS, 2, 2)),
            dma((2, GROUPS)),
            dma((RB,)),
            dma((RB,)),
            dma((3,)),
        ],
        compiler_params=pltpu.CompilerParams(
            collective_id=0, has_side_effects=True, vmem_limit_bytes=40 << 20
        ),
        name="gather_and_square",
    )(x, x_cols, c_cols, c_keep)


def on_device(x_blocks, x_cols, c_cols, c_keep):
    return square(x_blocks.reshape(RB, BLK, 128), x_cols.T, c_cols.T, c_keep.T)


def solution(mesh):
    spec = P("rows", "section")
    blocks = P("rows", "section", None, None, None)
    return jax.shard_map(
        on_device, mesh=mesh, in_specs=(blocks, spec, spec, spec), out_specs=blocks, check_vma=False
    )
```

```python
import jax
import jax.numpy as jnp
from jax import lax
from jax.experimental import pallas as pl
from jax.experimental.pallas import tpu as pltpu
from jax.sharding import PartitionSpec as P

MESH = pl.DeviceIdType.MESH
NX, NY, NZ, NC = 4, 4, 8, 2
RB = 12
GROUPS = 16
BLK = 256
HALF = RB // 2
META = 8
LC = 3
SLOTS = 16
SENDS = 194


def where_am_i():
    r, s = lax.axis_index("rows"), lax.axis_index("section")
    c = lax.rem(r, 2)
    y = lax.rem(r // 2, NY)
    x = lax.rem(s, 2) * 2 + r // 8
    return x, y, s // 2, c


def device(x, y, z, c):
    return ((lax.rem(x, 2) * NY + y) * 2 + c, z * 2 + x // 2)


def wrap(v, n):
    return lax.rem(v + n, n)


class Copies:
    def __init__(self, send):
        self.send, self.used, self.pending = send, 0, []

    def start(self, cond, src, dst, recv, to):
        copy = pltpu.make_async_remote_copy(
            src_ref=src, dst_ref=dst, send_sem=self.send.at[self.used], recv_sem=recv,
            device_id=to, device_id_type=MESH,
        )
        self.used += 1
        if cond is None:
            copy.start()
        else:
            pl.when(cond)(copy.start)
        self.pending.append((cond, copy))

    def finish(self):
        for cond, copy in self.pending:
            if cond is None:
                copy.wait_send()
            else:
                pl.when(cond)(copy.wait_send)


def enter(partners):
    barrier = pltpu.get_barrier_semaphore()
    for to in partners:
        pl.semaphore_signal(barrier, inc=1, device_id=to, device_id_type=MESH)
    pl.semaphore_wait(barrier, len(partners))


def square_kernel(
    x_ref, xc_ref, cc_ref, ck_ref, o_ref, a_ref, b_ref, am_ref, bm_ref, m_ref, c_ref, tab_v, tab_s,
    send, recv_a, recv_b, recv_m, send_c, recv_c, local,
):
    x, y, z, c = where_am_i()
    h = x // 2
    home = c == h
    away = c != h
    xp, xm = wrap(x + 1, NX), wrap(x - 1, NX)
    yp, ym, y2 = wrap(y + 1, NY), wrap(y - 1, NY), wrap(y + 2, NY)
    zp, zm = wrap(z + 1, NZ), wrap(z - 1, NZ)
    sib = device(x, y, z, 1 - c)
    swap = device(wrap(x + 2, NX), y, z, 1 - c)
    to_xp, to_xm = device(xp, y, z, c), device(xm, y, z, c)
    to_yp, to_ym = device(x, yp, z, c), device(x, ym, z, c)
    to_zp, to_zm = device(x, y, zp, c), device(x, y, zm, c)
    here = lax.rem(x, 2)

    def group(lo, ys, core):
        return (lo * NY + ys) * 2 + core

    own = group(here, y, c)
    a_own = 2 * z + c
    a_partner = 2 * z + (1 - c)

    mine = [
        pltpu.make_async_copy(x_ref, a_ref.at[a_own], local.at[0]),
        pltpu.make_async_copy(x_ref, b_ref.at[own], local.at[1]),
    ]

    @pl.when(home)
    def _():
        for copy in mine:
            copy.start()

    m_ref[...] = jnp.full((META, 128), -1, jnp.int32)
    m_ref[0:1, 0:RB] = xc_ref[...]
    m_ref[1 : 1 + LC, 0:RB] = jnp.where(ck_ref[...] != 0, cc_ref[...], -2)

    @pl.when(home)
    def _():
        am_ref[a_own] = m_ref[...]
        bm_ref[own] = m_ref[...]

    enter([sib, swap, device(wrap(x + 2, NX), y, z, c), to_xp, to_xm, to_yp, to_ym, to_zp, to_zm])
    cp = Copies(send)

    def wait_for(cond, view, sem):
        wait = pltpu.make_async_remote_copy(
            src_ref=view, dst_ref=view, send_sem=send.at[0], recv_sem=sem, device_id=sib, device_id_type=MESH
        ).wait_recv
        if cond is None:
            wait()
        else:
            pl.when(cond)(wait)

    def a_view(slot, core, k):
        rows = HALF if k is None else HALF // 2
        return a_ref.at[slot, pl.ds(core * HALF + (k or 0) * rows, rows)]

    def a_send(cond, slot, to, k=None):
        if k != 1:
            cp.start(cond, am_ref.at[slot], am_ref.at[slot], recv_m.at[0, slot], to)
        cp.start(cond, a_view(slot, c, k), a_view(slot, c, k), recv_a.at[slot, k or 0], to)

    def a_sib(cond, slot, k=None):
        cp.start(cond, a_view(slot, c, k), a_view(slot, c, k), recv_a.at[slot, 2 + (k or 0)], sib)

    def a_wait(cond, slot, k=None):
        wait_for(cond, a_view(slot, c, k), recv_a.at[slot, k or 0])
        if k != 1:
            wait_for(cond, am_ref.at[slot], recv_m.at[0, slot])

    def a_wait_sib(cond, slot, k=None):
        wait_for(cond, a_view(slot, 1 - c, k), recv_a.at[slot, 2 + (k or 0)])

    def b_view(slot, unit, k):
        _, first, rows, _ = unit
        if k is not None:
            rows = rows // 2
            first = first + k * rows
        return b_ref.at[slot, pl.ds(first, rows)]

    def b_send(cond, slot, unit, to, k=None):
        if k != 1 and unit[3] == 0:
            cp.start(cond, bm_ref.at[slot], bm_ref.at[slot], recv_m.at[1, slot], to)
        cp.start(cond, b_view(slot, unit, k), b_view(slot, unit, k), recv_b.at[slot, unit[3], k or 0], to)

    def b_wait(cond, slot, unit, k=None):
        wait_for(cond, b_view(slot, unit, k), recv_b.at[slot, unit[3], k or 0])
        if k != 1 and unit[3] == 0:
            wait_for(cond, bm_ref.at[slot], recv_m.at[1, slot])

    x_first = [(0, 0, RB, 0), (1, 0, 2, 0)]
    y_first = (1, 2, RB - 2, 1)

    for core in (0, 1):
        to = device(wrap(x + 2, NX), y, z, core)
        cp.start(away, m_ref, am_ref.at[a_partner], recv_m.at[0, a_partner], to)
        cp.start(away, x_ref.at[pl.ds(core * HALF, HALF)], a_view(a_partner, core, None), recv_a.at[a_partner, 0], to)
    cp.start(away, m_ref, bm_ref.at[own], recv_m.at[1, own], sib)
    cp.start(away, x_ref, b_ref.at[own], recv_b.at[own, 0, 0], sib)

    @pl.when(home)
    def _():
        for copy in mine:
            copy.wait()

    def z_own(cond, slot):
        for to in (to_zp, to_zm):
            a_send(cond, slot, to)

    a_first, a_swapped = 2 * z + h, 2 * z + 1 - h
    cp.start(home, am_ref.at[a_first], am_ref.at[a_first], recv_m.at[0, a_first], sib)
    cp.start(home, a_view(a_first, 1 - c, None), a_view(a_first, 1 - c, None), recv_a.at[a_first, 0], sib)
    z_own(home, a_first)
    a_sib(home, a_first)
    a_wait(away, a_first)
    z_own(away, a_first)
    from_sib = group(here, y, 1 - c)
    wait_for(home, b_ref.at[from_sib], recv_b.at[from_sib, 0, 0])
    wait_for(home, bm_ref.at[from_sib], recv_m.at[1, from_sib])

    def x_sends(cond, slot, unit):
        for to in (to_xp, to_xm):
            b_send(cond, slot, unit, to)

    def y_sends(cond, slot, unit):
        for to in (to_yp, to_ym):
            b_send(cond, slot, unit, to)

    js = [wrap(x - 2 * c - lo, NX) for lo in (0, 1)]
    beside = [(j == 1) | (j == 3) for j in js]

    def x_pass(cond, lo, ys, unit):
        slot = group(lo, ys, unit[0])
        for jj, k, to in ((1, 0, to_xp), (3, 1, to_xm)):
            on = cond & (js[lo] == jj)
            b_wait(on, slot, unit)
            b_send(on, slot, unit, to, k)

    def x_end(lo, ys, unit):
        for k in (0, 1):
            b_wait(js[lo] == 2, group(lo, ys, unit[0]), unit, k)

    def y_pass(cond, lo, unit):
        for ys, k, to in ((ym, 0, to_yp), (yp, 1, to_ym)):
            slot = group(lo, ys, unit[0])
            b_wait(cond, slot, unit)
            b_send(cond, slot, unit, to, k)

    def y_end(cond, lo, unit):
        for k in (0, 1):
            b_wait(cond, group(lo, y2, unit[0]), unit, k)

    def ring(d):
        for par in (h, 1 - h):
            for zs, k, to in ((wrap(z - d, NZ), 0, to_zp), (wrap(z + d, NZ), 1, to_zm)):
                slot = 2 * zs + par
                a_wait(None, slot)
                a_send(None, slot, to, k if d == 3 else None)
                a_sib(None, slot)

    x_sends(home, group(here, y, 0), x_first[0])
    y_sends(home, group(here, y, 1), y_first)
    x_sends(home, group(here, y, 1), x_first[1])
    y_sends(home, group(here, y, 0), x_first[0])
    y_sends(home, group(here, y, 1), x_first[1])
    x_sends(home, group(here, y, 1), y_first)

    a_wait(None, a_swapped)
    z_own(None, a_swapped)
    a_sib(None, a_swapped)
    for lo in (0, 1):
        x_pass(True, lo, y, x_first[0])
        y_sends(away & beside[lo], group(lo, y, 0), x_first[0])
    for lo in (0, 1):
        x_pass(True, lo, y, x_first[1])
        y_sends(away & beside[lo], group(lo, y, 1), x_first[1])
    y_pass(home, here, y_first)
    for ys in (ym, yp):
        x_sends(home, group(here, ys, 1), y_first)
    ring(1)
    for lo in (0, 1):
        x_end(lo, y, x_first[0])
        y_sends(js[lo] == 2, group(lo, y, 0), x_first[0])
    for lo in (0, 1):
        x_end(lo, y, x_first[1])
        y_sends(js[lo] == 2, group(lo, y, 1), x_first[1])
    y_end(home, here, y_first)
    x_sends(home, group(here, y2, 1), y_first)
    ring(2)
    for unit in x_first:
        for lo in (0, 1):
            y_sends(home & beside[lo], group(lo, y, unit[0]), unit)
    for lo in (0, 1):
        y_pass(away, lo, x_first[0])
    for lo in (0, 1):
        y_pass(away, lo, x_first[1])
    for unit in x_first:
        y_pass(home, here, unit)
    for lo in (0, 1):
        x_pass(True, lo, y, y_first)
    for lo in (0, 1):
        x_pass(True, lo, ym, y_first)
    for lo in (0, 1):
        x_pass(True, lo, yp, y_first)
    ring(3)
    for lo in (0, 1):
        x_pass(True, lo, y2, y_first)
    for unit in x_first:
        for lo in (0, 1):
            y_end(away, lo, unit)
    for ys in (y, ym, yp, y2):
        for lo in (0, 1):
            x_end(lo, ys, y_first)
    for unit in x_first:
        for lo in (0, 1):
            y_pass(home & beside[lo], lo, unit)

    for par in (h, 1 - h):
        slot = 2 * wrap(z + 4, NZ) + par
        for k in (0, 1):
            a_wait(None, slot, k)
            a_sib(None, slot, k)
    a_wait_sib(away, a_first)
    a_wait_sib(None, a_swapped)
    for d in range(1, NZ):
        for par in (h, 1 - h):
            for k in (0, 1) if d == 4 else (None,):
                a_wait_sib(None, 2 * wrap(z + d, NZ) + par, k)

    for unit in x_first:
        for lo in (0, 1):
            y_end(home, lo, unit)

    order = [group(lo, ys, core) for ys in (y, ym, yp, y2) for lo in (0, 1) for core in (0, 1)]
    sub = lax.broadcasted_iota(jnp.int32, (SLOTS, 128), 0)
    lane = lax.broadcasted_iota(jnp.int32, (SLOTS, 128), 1)

    def upright(row):
        return jnp.sum(jnp.where(lane == sub, row, 0), axis=1, keepdims=True)

    def look_up(places):
        wanted = [upright(am_ref[a_own, pl.ds(1 + q, 1), :]) for q in range(LC)]
        blocks = codes = jnp.zeros((SLOTS, 128), jnp.int32)
        for p in places:
            t = order[p]
            col = upright(am_ref[t, pl.ds(0, 1), :])
            far = jnp.sum(jnp.where(lane == col, bm_ref[t, pl.ds(0, 1), :] + 1, 0), axis=1, keepdims=True) - 1
            code = jnp.zeros_like(col)
            for q in range(LC):
                code = code + jnp.where((col >= 0) & (far >= 0) & (far == wanted[q]), q + 1, 0)
            blocks = jnp.where(lane == p, jnp.maximum(col, 0), blocks)
            codes = jnp.where(lane == p, code, codes)
        tab_v[0] = blocks
        tab_v[1] = codes
        to_smem = pltpu.make_async_copy(tab_v.at[0], tab_s, local.at[2])
        to_smem.start()
        to_smem.wait()

    def multiply(i, places, total):
        row_codes = tab_v[1, pl.ds(i, 1), :]
        masks = [jnp.where(row_codes == k + 1, 1.0, 0.0).astype(jnp.bfloat16) for k in range(LC)]
        for p in places:
            t = order[p]
            a = a_ref[t, i]
            lhs = jnp.concatenate([a[:128], a[128:]], axis=1)
            lhs = jnp.concatenate([lhs * masks[k][:, p : p + 1] for k in range(LC)], axis=0)
            b = b_ref[t, tab_s[i, p]]
            rhs = jnp.concatenate(
                [jnp.concatenate([b[:128], b[128:]], axis=1), jnp.concatenate([-b[128:], b[:128]], axis=1)], axis=0
            )
            term = jnp.dot(lhs, rhs, preferred_element_type=jnp.float32)
            total = term if total is None else total + term
        return total

    def finish_row(i, total):
        for k in range(LC):
            for p in (0, 1):
                c_ref[i, k, p] = total[128 * k : 128 * (k + 1), 128 * p : 128 * (p + 1)].astype(jnp.bfloat16)

    def moved(i):
        return pltpu.make_async_remote_copy(
            src_ref=c_ref.at[i], dst_ref=o_ref.at[i], send_sem=send_c.at[i], recv_sem=recv_c.at[i],
            device_id=swap, device_id_type=MESH,
        )

    def stored(i):
        return pltpu.make_async_copy(c_ref.at[i], o_ref.at[i], send_c.at[i])

    look_up(range(GROUPS))

    @pl.loop(0, RB)
    def _(i):
        finish_row(i, multiply(i, range(GROUPS), None))

        @pl.when(away)
        def _():
            moved(i).start()

        @pl.when(home)
        def _():
            stored(i).start()

    @pl.loop(0, RB)
    def _(i):
        @pl.when(away)
        def _():
            moved(i).wait()

        @pl.when(home)
        def _():
            stored(i).wait()

    cp.finish()


def square(x, x_cols, c_cols, c_keep):
    dma = pltpu.SemaphoreType.DMA
    vmem = pltpu.VMEM
    return pl.pallas_call(
        square_kernel,
        out_shape=jax.ShapeDtypeStruct((RB, LC, 2, 128, 128), jnp.bfloat16),
        in_specs=[pl.BlockSpec(memory_space=pltpu.HBM)] + [pl.BlockSpec(memory_space=vmem)] * 3,
        out_specs=pl.BlockSpec(memory_space=pl.ANY),
        scratch_shapes=[
            vmem((GROUPS, RB, BLK, 128), jnp.bfloat16),
            vmem((GROUPS, RB, BLK, 128), jnp.bfloat16),
            vmem((GROUPS, META, 128), jnp.int32),
            vmem((GROUPS, META, 128), jnp.int32),
            vmem((META, 128), jnp.int32),
            vmem((RB, LC, 2, 128, 128), jnp.bfloat16),
            vmem((2, SLOTS, 128), jnp.int32),
            pltpu.SMEM((SLOTS, 128), jnp.int32),
            dma((SENDS,)),
            dma((GROUPS, 4)),
            dma((GROUPS, 2, 2)),
            dma((2, GROUPS)),
            dma((RB,)),
            dma((RB,)),
            dma((3,)),
        ],
        compiler_params=pltpu.CompilerParams(
            collective_id=0, has_side_effects=True, vmem_limit_bytes=40 << 20
        ),
        name="gather_and_square",
    )(x, x_cols, c_cols, c_keep)


def on_device(x_blocks, x_cols, c_cols, c_keep):
    return square(x_blocks.reshape(RB, BLK, 128), x_cols.T, c_cols.T, c_keep.T)


def solution(mesh):
    spec = P("rows", "section")
    blocks = P("rows", "section", None, None, None)
    return jax.shard_map(
        on_device, mesh=mesh, in_specs=(blocks, spec, spec, spec), out_specs=blocks, check_vma=False
    )
```
